32 devices in a mesh: section: 2 (over x), tile: 8 (over z, core), slide: 2 (over y).
Axes of the slice: x: 2, y: 2, z: 4, core: 2. Of those that a mesh axis runs over, the one named last changes fastest.
Arguments:
- features: bfloat16 [2, 16384, 2048], P('slide', ('section', 'tile')), may hold values from -6 to 6
- w_proj: bfloat16 [2048, 1024], P(('section', 'tile', 'slide')), may hold values from -0.25 to 0.25
- w_fc: bfloat16 [1024, 128], replicated, may hold values from -0.1875 to 0.1875
- w_up: bfloat16 [3, 128, 256], replicated, may hold values from -0.5 to 0.5
- w_down: bfloat16 [3, 256, 128], replicated, may hold values from -0.375 to 0.375
- self_adj: bfloat16 [2, 128, 128, 128], P('slide', ('section', 'tile')), may hold values from -0.1875 to 0.1875
- adjacency: bfloat16 [2, 128, 8, 128, 128], P('slide', ('section', 'tile')), may hold values from -0.1875 to 0.1875
- nbr_block: int32 [2, 128, 8], P('slide'), may hold values from 0 to 127, as said below
- counts: int32 [2, 128], P('slide', ('section', 'tile')), may hold values from 6 to 8
Outputs:
- node_out: bfloat16 [2, 16384, 128], P('slide', ('section', 'tile'))
The draws below stay inside these ranges and needn't reach their ends.
Inputs may be any that keep to these rules, and one draw needn't show every extreme that they name: `nbr_block`: block g of a slide is the (g % 8)-th block of the (g // 8)-th group of 8 blocks. Among the 64 entries of one such group, at most 4 name blocks of any one group, and some group is named exactly 4 times; slots beyond counts are named too.
All inputs are finite; a program needn't handle non-finite values.
Results may differ from the reference program's by a relative error of at most 0.015.
Values may be sent and summed in bfloat16 or wider, within the bound.
A program may use at most 64 MiB of HBM per device.

```python
import jax
import jax.numpy as jnp
from jax import lax

F_IN = 2048
F_MID = 1024
H = 128
HID2 = 256
TB = 128
KNB = 8
HOPS = 3
BLK_DEV = 8
SLIDES = 2
NBLK = 128
TILES = 16384


def draw_nbr_block(key, part):
    groups = NBLK // BLK_DEV
    sends = BLK_DEV * KNB
    first, second, third = jax.random.split(key, 3)
    order = jax.vmap(lambda k: jax.random.permutation(k, groups))(jax.random.split(first, SLIDES * groups))
    order = order.reshape(SLIDES, groups, groups)
    shuffle = jax.vmap(lambda k: jax.random.permutation(k, sends))(jax.random.split(second, SLIDES * groups))
    shuffle = shuffle.reshape(SLIDES, groups, sends)
    target = jnp.take_along_axis(order, shuffle % groups, axis=2)
    local = jax.random.randint(third, (SLIDES, groups, sends), 0, BLK_DEV)
    return (target * BLK_DEV + local).reshape(SLIDES, NBLK, KNB).astype(jnp.int32)


def set_ends(result, stream_key, smallest, largest):
    index_at = [jax.random.randint(jax.random.fold_in(stream_key, axis), (), 0, length) for axis, length in enumerate(result.shape)]
    longest = result.shape.index(max(result.shape))
    beside = index_at[:longest] + [(index_at[longest] + 1) % result.shape[longest]] + index_at[longest + 1:]
    return result.at[tuple(index_at)].set(smallest).at[tuple(beside)].set(largest)


def spiked(entries, stream_key, source, target, parts, factor):
    owner, partner = [(jnp.arange(entries.shape[dim]) // (entries.shape[dim] // parts)).reshape([-1 if axis == dim else 1 for axis in range(entries.ndim)]) for dim in (source, target)]
    chosen = jax.random.permutation(stream_key, parts)[partner]
    strong = (owner == chosen) | (owner == (partner + parts // 2) % parts)
    return jnp.where(strong, factor * entries, entries)


def level_of(key, dims, cuts, low, largest):
    gain, own = 1.0, jax.random.fold_in(key, 6)
    for position, shards_of in cuts:
        draws = jnp.exp(jax.random.uniform(jax.random.fold_in(own, position), (shards_of,), jnp.float32, low / len(cuts), largest / len(cuts)))
        gain = gain * jnp.repeat(draws, dims[position] // shards_of).reshape([-1 if axis == position else 1 for axis in range(len(dims))])
    return gain


def centred(own_key, extent, scale, bound, cuts=(), dtype=jnp.bfloat16):
    entries = jax.random.normal(own_key, extent, jnp.float32) * scale
    if len(cuts) > 0:
        entries = level_of(own_key, extent, cuts, -0.22, 0.18) * entries
    return jnp.clip(entries, min=-bound, max=bound).astype(dtype)


def bell_draw_with(stream_key, dims, spread, most, cuts, heavy, held_as=jnp.bfloat16):
    drawn = spread * jax.random.normal(stream_key, dims, jnp.float32)
    if cuts:
        drawn = drawn * level_of(stream_key, dims, cuts, -0.22, 0.18)
    return jnp.clip(spiked(drawn, jax.random.fold_in(stream_key, 3), *heavy), -most, most).astype(held_as)


def setup_inputs(seed: int = 0) -> dict:
    seeds = jax.random.split(jax.random.key(seed), 10)
    return {
        "features": centred(seeds[0], (SLIDES, TILES, F_IN), 1.0, 6.0, ((0, 2), (1, 16))),
        "w_proj": bell_draw_with(seeds[1], (F_IN, F_MID), F_IN ** -0.5, 0.25, ((0, 32),), (0, 1, 32, 2.75)),
        "w_fc": centred(seeds[2], (F_MID, H), F_MID ** -0.5, 0.1875),
        "w_up": centred(seeds[3], (HOPS, H, HID2), H ** -0.5, 0.5),
        "w_down": centred(seeds[4], (HOPS, HID2, H), HID2 ** -0.5, 0.375),
        "self_adj": centred(seeds[5], (SLIDES, NBLK, TB, TB), ((TB * (KNB + 1)) ** -0.5), 0.1875, ((0, 2), (1, 16))),
        "adjacency": centred(seeds[6], (SLIDES, NBLK, KNB, TB, TB), ((TB * (KNB + 1)) ** -0.5), 0.1875, ((0, 2), (1, 16))),
        "nbr_block": draw_nbr_block(jax.random.fold_in(seeds[9], 71), 0),
        "counts": set_ends(jax.random.randint(seeds[8], (SLIDES, NBLK), KNB - 2, KNB + 1), jax.random.fold_in(seeds[8], 1), KNB - 2, KNB).astype(jnp.int32),
    }


def one_slide(features, w_proj, w_fc, w_up, w_down, self_adj, adjacency, nbr_block, counts):
    pre = jnp.dot(features, w_proj, preferred_element_type=jnp.float32)
    encoded = jax.nn.relu(pre).astype(jnp.bfloat16)
    state = jnp.dot(encoded, w_fc, preferred_element_type=jnp.float32)
    live = jnp.arange(KNB).astype(jnp.int32)[None, :] < counts[:, None]
    for hop in range(HOPS):
        nodes = state.astype(jnp.bfloat16).reshape(NBLK, TB, H)
        own = jnp.einsum("bij,bjh->bih", self_adj.astype(jnp.float32), nodes.astype(jnp.float32))

        def push(total, item):
            block_adj, block_nodes, targets, flags = item
            piece = jnp.einsum("kij,jh->kih", block_adj.astype(jnp.float32), block_nodes.astype(jnp.float32))
            piece = jnp.where(flags[:, None, None], piece, 0.0).astype(jnp.bfloat16)
            return total.at[targets.astype(jnp.int32)].add(piece.astype(jnp.float32)), None

        incoming, unused = lax.scan(push, jnp.zeros((NBLK, TB, H), jnp.float32), (adjacency, nodes, nbr_block, live))
        gathered = (own + incoming).astype(jnp.bfloat16).reshape(TILES, H)
        inner = jax.nn.relu(jnp.dot(gathered, w_up[hop], preferred_element_type=jnp.float32)).astype(jnp.bfloat16)
        state = state + jnp.dot(inner, w_down[hop], preferred_element_type=jnp.float32)
    return state.astype(jnp.bfloat16)


def reference(features, w_proj, w_fc, w_up, w_down, self_adj, adjacency, nbr_block, counts):
    results = [one_slide(features[slide_idx], w_proj, w_fc, w_up, w_down, self_adj[slide_idx], adjacency[slide_idx], nbr_block[slide_idx], counts[slide_idx]) for slide_idx in range(SLIDES)]
    return jnp.stack(results)
```

```python
import functools

import jax
import jax.numpy as jnp
from jax import lax
from jax.experimental import pallas as pl
from jax.experimental.pallas import tpu as pltpu
from jax.sharding import PartitionSpec as P

MESH = pl.DeviceIdType.MESH
CORES = 2
BF = jnp.bfloat16
F32 = jnp.float32


def remote(src, dst, send_sem, recv_sem, device):
    return pltpu.make_async_remote_copy(
        src_ref=src,
        dst_ref=dst,
        send_sem=send_sem,
        recv_sem=recv_sem,
        device_id=device,
        device_id_type=MESH,
    )


def near_first(count):
    order = [0]
    for step in range(1, count // 2 + 1):
        order += [step] if step == count - step else [step, count - step]
    return order


def greet(devices):
    barrier = pltpu.get_barrier_semaphore()
    for device in devices:
        pl.semaphore_signal(barrier, inc=1, device_id=device, device_id_type=MESH)
    return lambda: pl.semaphore_wait(barrier, len(devices))


def encode_kernel(tiles, x_ref, w_ref, fc_ref, out_ref, w_all, acc, z_s, z_r, xy_s, xy_r, dg_s, dg_r, pt_s, pt_r):
    zs = tiles // CORES
    rows = w_ref.shape[0]
    half = rows // 2
    sx = lax.axis_index("section")
    sy = lax.axis_index("slide")
    t = lax.axis_index("tile")
    z, c = t // CORES, t % CORES
    ox, oy, oc = 1 - sx, 1 - sy, 1 - c
    partner = {"tile": z * CORES + oc}
    xn, yn = {"section": ox}, {"slide": oy}

    def zdev(o):
        return {"tile": ((z + o) % zs) * CORES + c}

    def at(x, o, core, y, part=None):
        zz = (z + o) % zs
        start = ((x * tiles + zz * CORES + core) * 2 + y) * rows
        if part is None:
            return w_all.at[pl.ds(pl.multiple_of(start, rows), rows)]
        return w_all.at[pl.ds(pl.multiple_of(start + part * half, half), half)]

    started = []

    def go(src, dst, ss, rs, device):
        copy = remote(src, dst, ss, rs, device)
        copy.start()
        started.append(copy)

    def arrived(dst, ss, rs, device):
        remote(dst, dst, ss, rs, device).wait_recv()

    wait = greet([partner, xn, yn] + [zdev(o) for o in range(1, zs)])
    start = ((sx * tiles + t) * 2 + sy) * rows
    w_all[pl.ds(pl.multiple_of(start, rows), rows)] = w_ref[...]
    wait()

    order = near_first(zs)
    for o in order[1:]:
        go(w_ref, at(sx, 0, c, sy), z_s.at[o], z_r.at[o], zdev(o))

    def line(o):
        src = w_ref if o == 0 else at(sx, o, c, sy)
        if o:
            arrived(src, z_s.at[0], z_r.at[zs - o], zdev(o))
        here = at(sx, o, c, sy)
        go(src, here, xy_s.at[0, o], xy_r.at[0, o], xn)
        go(src, here, xy_s.at[1, o], xy_r.at[1, o], yn)
        go(src, here, pt_s.at[0, o], pt_r.at[0, o], partner)

    def cross(o):
        ref = at(ox, o, c, sy)
        arrived(ref, xy_s.at[0, o], xy_r.at[0, o], xn)
        part = at(ox, o, c, sy, 0)
        go(part, part, dg_s.at[0, o], dg_r.at[0, o], yn)
        go(ref, ref, pt_s.at[1, o], pt_r.at[1, o], partner)
        ref = at(sx, o, c, oy)
        arrived(ref, xy_s.at[1, o], xy_r.at[1, o], yn)
        part = at(sx, o, c, oy, 1)
        go(part, part, dg_s.at[1, o], dg_r.at[1, o], xn)
        go(ref, ref, pt_s.at[2, o], pt_r.at[2, o], partner)

    def corner(o):
        for k, device in enumerate((yn, xn)):
            part = at(ox, o, c, oy, k)
            arrived(part, dg_s.at[k, o], dg_r.at[k, o], device)
            go(part, part, pt_s.at[3 + k, o], pt_r.at[3 + k, o], partner)

    depth = CORES * 2 * rows

    def multiply(o, first):
        refs = [at(sx, o, oc, sy), at(ox, o, oc, sy), at(sx, o, oc, oy), at(ox, o, oc, oy, 0), at(ox, o, oc, oy, 1)]
        for k, ref in enumerate(refs):
            arrived(ref, pt_s.at[k, o], pt_r.at[k, o], partner)
        cols = [((x * zs) + (z + o) % zs) * depth for x in (sx, ox)]
        slabs = [pl.ds(pl.multiple_of(s, depth), depth) for s in cols]
        tall = x_ref.shape[0] // 4

        def body(i, carry):
            strip = pl.ds(pl.multiple_of(i * tall, tall), tall)
            total = jnp.dot(x_ref[strip, slabs[0]], w_all[slabs[0], :], preferred_element_type=F32)
            total += jnp.dot(x_ref[strip, slabs[1]], w_all[slabs[1], :], preferred_element_type=F32)
            acc[strip, :] = total if first else acc[strip, :] + total
            return carry

        lax.fori_loop(0, 4, body, 0)

    for step in range(zs + 3):
        if step < zs:
            line(order[step])
        if 0 <= step - 1 < zs:
            cross(order[step - 1])
        if 0 <= step - 2 < zs:
            corner(order[step - 2])
        if 0 <= step - 3 < zs:
            multiply(order[step - 3], step == 3)

    tall = x_ref.shape[0] // 4

    def finish(i, carry):
        strip = pl.ds(pl.multiple_of(i * tall, tall), tall)
        enc = jnp.maximum(acc[strip, :], 0.0).astype(BF)
        out_ref[strip, :] = jnp.dot(enc, fc_ref[...], preferred_element_type=F32)
        return carry

    lax.fori_loop(0, 4, finish, 0)
    for copy in started:
        copy.wait_send()


def encode(rows, w_proj, w_fc):
    tiles = lax.axis_size("tile")
    zs = tiles // CORES
    vmem = pl.BlockSpec(memory_space=pltpu.VMEM)
    dma = pltpu.SemaphoreType.DMA
    return pl.pallas_call(
        functools.partial(encode_kernel, tiles),
        out_shape=jax.ShapeDtypeStruct((rows.shape[0], w_fc.shape[1]), F32),
        in_specs=[vmem] * 3,
        out_specs=vmem,
        scratch_shapes=[
            pltpu.VMEM((rows.shape[1], w_proj.shape[1]), BF),
            pltpu.VMEM((rows.shape[0], w_proj.shape[1]), F32),
            dma((zs,)),
            dma((zs,)),
            dma((2, zs)),
            dma((2, zs)),
            dma((2, zs)),
            dma((2, zs)),
            dma((5, zs)),
            dma((5, zs)),
        ],
        compiler_params=pltpu.CompilerParams(
            collective_id=0, has_side_effects=True, vmem_limit_bytes=40 << 20
        ),
        name="encode",
    )(rows, w_proj, w_fc)


def hops_kernel(tiles, cap, list_ref, state_ref, adj_ref, self_ref, up_ref, down_ref, out_ref,
                state, terms, send0, own0, recv0, send1, recv1, send2, recv2, agg, s0, r0, s1, r1, s2, r2):
    hops = up_ref.shape[0]
    zs = tiles // CORES
    blocks, slots, tb, _ = adj_ref.shape
    width = state_ref.shape[1]
    sends = blocks * slots
    sx = lax.axis_index("section")
    t = lax.axis_index("tile")
    z, c = t // CORES, t % CORES
    ox, oc = 1 - sx, 1 - c
    partner = {"tile": z * CORES + oc}
    xn = {"section": ox}
    order = near_first(zs)
    order = order[:0:-1] + [0]

    def zdev(o):
        return {"tile": ((z + o) % zs) * CORES + c}

    wait = greet([partner, xn] + [zdev(o) for o in range(1, zs)])
    terms[sends] = jnp.zeros((tb, width), BF)
    state[...] = state_ref[...]

    for hop in range(hops):
        pending = []

        def go(src, dst, ss, rs, device):
            copy = remote(src, dst, ss, rs, device)
            copy.start()
            pending.append(copy)

        def term(b, carry):
            nodes = state[pl.ds(pl.multiple_of(b * tb, tb), tb), :].astype(BF)
            whole = jnp.dot(adj_ref[b].reshape(slots * tb, tb), nodes, preferred_element_type=F32)
            terms[pl.ds(b * slots, slots)] = whole.astype(BF).reshape(slots, tb, width)
            agg[pl.ds(pl.multiple_of(b * tb, tb), tb), :] = jnp.dot(self_ref[b], nodes, preferred_element_type=F32)
            return carry

        lax.fori_loop(0, blocks, term, 0)
        if hop == 0:
            wait()

        def sums(dst, x, o, core):
            first = ((x * zs + (z + o) % zs) * CORES + core) * blocks

            def body(r, carry):
                base = (first + r) * cap
                total = terms[list_ref[base]].astype(F32)
                for j in range(1, cap):
                    total += terms[list_ref[base + j]].astype(F32)
                dst[r] = total.astype(BF)
                return carry

            lax.fori_loop(0, blocks, body, 0)

        def chip(k, i):
            o = order[i]
            x = (ox, sx)[k]
            sums(send0.at[k, i], x, o, oc)
            go(send0.at[k, i], recv0.at[hop, k, i], s0.at[hop, k, i], r0.at[hop, k, i], partner)
            sums(own0.at[k, i], x, o, c)

        def pair(i):
            remote(recv0.at[hop, 0, i], recv0.at[hop, 0, i], s0.at[hop, 0, i], r0.at[hop, 0, i], partner).wait_recv()

            def body(r, carry):
                send1[i, r] = (own0[0, i, r].astype(F32) + recv0[hop, 0, i, r].astype(F32)).astype(BF)
                return carry

            lax.fori_loop(0, blocks, body, 0)
            go(send1.at[i], recv1.at[hop, i], s1.at[hop, i], r1.at[hop, i], xn)

        chip(0, 0)
        for i in range(1, zs):
            chip(0, i)
            pair(i - 1)
        chip(1, 0)
        pair(zs - 1)
        for i in range(1, zs):
            chip(1, i)

        for i in range(zs):
            remote(recv0.at[hop, 1, i], recv0.at[hop, 1, i], s0.at[hop, 1, i], r0.at[hop, 1, i], partner).wait_recv()
            remote(recv1.at[hop, i], recv1.at[hop, i], s1.at[hop, i], r1.at[hop, i], xn).wait_recv()
            o = order[i]

            def body(r, carry):
                total = own0[1, i, r].astype(F32) + recv0[hop, 1, i, r].astype(F32)
                total += recv1[hop, i, r].astype(F32)
                if o:
                    send2[o - 1, r] = total.astype(BF)
                else:
                    agg[pl.ds(pl.multiple_of(r * tb, tb), tb), :] += total
                return carry

            lax.fori_loop(0, blocks, body, 0)
            if o:
                go(send2.at[o - 1], recv2.at[hop, o - 1], s2.at[hop, o - 1], r2.at[hop, o - 1], zdev(o))
        for o in order[:-1]:
            remote(recv2.at[hop, o - 1], recv2.at[hop, o - 1], s2.at[hop, o - 1], r2.at[hop, o - 1], zdev(o)).wait_recv()

        def mlp(r, carry):
            strip = pl.ds(pl.multiple_of(r * 2 * tb, 2 * tb), 2 * tb)
            total = agg[strip, :]
            for o in range(1, zs):
                total += recv2[hop, o - 1, pl.ds(r * 2, 2)].astype(F32).reshape(2 * tb, width)
            inner = jnp.dot(total.astype(BF), up_ref[hop], preferred_element_type=F32)
            inner = jnp.maximum(inner, 0.0).astype(BF)
            after = state[strip, :] + jnp.dot(inner, down_ref[hop], preferred_element_type=F32)
            state[strip, :] = after
            if hop == hops - 1:
                out_ref[strip, :] = after.astype(BF)
            return carry

        lax.fori_loop(0, blocks // 2, mlp, 0)
        for copy in pending:
            copy.wait_send()


def graph(state, adjacency, self_adj, w_up, w_down, lists, cap):
    tiles = lax.axis_size("tile")
    zs = tiles // CORES
    blocks, slots, tb, _ = adjacency.shape
    width = state.shape[1]
    hops = w_up.shape[0]
    piece = (blocks, tb, width)
    vmem = pl.BlockSpec(memory_space=pltpu.VMEM)
    dma = pltpu.SemaphoreType.DMA
    return pl.pallas_call(
        functools.partial(hops_kernel, tiles, cap),
        out_shape=jax.ShapeDtypeStruct(state.shape, BF),
        in_specs=[pl.BlockSpec(memory_space=pltpu.SMEM)] + [vmem] * 5,
        out_specs=vmem,
        scratch_shapes=[
            pltpu.VMEM(state.shape, F32),
            pltpu.VMEM((blocks * slots + 1, tb, width), BF),
            pltpu.VMEM((2, zs) + piece, BF),
            pltpu.VMEM((2, zs) + piece, BF),
            pltpu.VMEM((hops, 2, zs) + piece, BF),
            pltpu.VMEM((zs,) + piece, BF),
            pltpu.VMEM((hops, zs) + piece, BF),
            pltpu.VMEM((zs - 1,) + piece, BF),
            pltpu.VMEM((hops, zs - 1) + piece, BF),
            pltpu.VMEM(state.shape, F32),
            dma((hops, 2, zs)),
            dma((hops, 2, zs)),
            dma((hops, zs)),
            dma((hops, zs)),
            dma((hops, zs)),
            dma((hops, zs)),
        ],
        compiler_params=pltpu.CompilerParams(
            collective_id=1, has_side_effects=True, vmem_limit_bytes=50 << 20
        ),
        name="hops",
    )(lists, state, adjacency, self_adj, w_up, w_down)


def entry_lists(targets, live, total_blocks, cap):
    sends = targets.shape[0]
    positions = jnp.arange(sends, dtype=jnp.int32)
    same = (targets[:, None] == targets[None, :]) & live[None, :] & (positions[None, :] < positions[:, None])
    rank = jnp.sum(same.astype(jnp.int32), axis=1)
    hit = (jnp.arange(total_blocks, dtype=jnp.int32)[:, None, None] == targets[None, None, :]) & live[None, None, :]
    hit = hit & (jnp.arange(cap, dtype=jnp.int32)[None, :, None] == rank[None, None, :])
    found = jnp.sum(jnp.where(hit, positions[None, None, :] - sends, 0), axis=2) + sends
    return found.reshape(total_blocks * cap)


def local(features, w_proj, w_fc, w_up, w_down, self_adj, adjacency, nbr_block, counts):
    rows = features[0]
    blocks = self_adj.shape[1]
    tb = self_adj.shape[2]
    width = w_fc.shape[1]
    slots = adjacency.shape[2]
    hops = w_up.shape[0]
    pairs = lax.axis_size("section") == 2 and lax.axis_size("tile") % CORES == 0
    peers = lax.axis_size("section") * lax.axis_size("tile")
    me_index = lax.axis_index("section") * lax.axis_size("tile") + lax.axis_index("tile")
    sends = blocks * slots
    cap = (sends + peers - 1) // peers
    if pairs and lax.axis_size("slide") == 2 and w_proj.shape[0] % 32 == 0:
        state = encode(rows, w_proj, w_fc)
    else:
        pre = jnp.dot(
            rows,
            lax.all_gather(w_proj, ("section", "tile", "slide"), axis=0, tiled=True),
            preferred_element_type=F32,
        )
        encoded = jax.nn.relu(pre).astype(BF)
        state = jnp.dot(encoded, w_fc, preferred_element_type=F32)
    live = jnp.arange(slots, dtype=jnp.int32)[None, :] < counts[0][:, None]
    if pairs and blocks <= CORES * cap:
        targets = lax.dynamic_slice_in_dim(nbr_block[0], me_index * blocks, blocks, 0).reshape(sends)
        lists = entry_lists(targets, live.reshape(sends), peers * blocks, cap)
        return graph(state, adjacency[0], self_adj[0], w_up, w_down, lists, cap)[None]
    table = nbr_block[0].reshape(peers, sends)
    target_dev = table // blocks
    target_local = table % blocks
    positions = jnp.arange(sends, dtype=jnp.int32)
    before = positions[None, :] < positions[:, None]
    same = target_dev[:, :, None] == target_dev[:, None, :]
    ranking = jnp.sum(jnp.logical_and(same, before[None]).astype(jnp.int32), axis=2)
    mine_dev = lax.dynamic_index_in_dim(target_dev, me_index, 0, keepdims=False)
    mine_rank = lax.dynamic_index_in_dim(ranking, me_index, 0, keepdims=False)
    slot_of = mine_dev * cap + mine_rank
    send_map = (jnp.arange(peers * cap, dtype=jnp.int32)[:, None] == slot_of[None, :]).astype(BF)
    arrive_hit = target_dev == me_index
    slot_flags = jnp.logical_and(
        arrive_hit[:, :, None],
        ranking[:, :, None] == jnp.arange(cap, dtype=jnp.int32)[None, None, :],
    ).astype(F32)
    local_flags = (
        target_local[:, :, None] == jnp.arange(blocks, dtype=jnp.int32)[None, None, :]
    ).astype(F32)
    recv_map = (
        jnp.einsum("pjc,pjr->rpc", slot_flags, local_flags).reshape(blocks, peers * cap).astype(BF)
    )
    for hop in range(hops):
        nodes = state.astype(BF).reshape(blocks, tb, width)
        own = jnp.einsum("bij,bjh->bih", self_adj[0], nodes, preferred_element_type=F32)
        terms = jnp.einsum("bkij,bjh->bkih", adjacency[0], nodes, preferred_element_type=F32)
        terms = (
            jnp.where(live[:, :, None, None], terms, 0.0).astype(BF).reshape(sends, tb * width)
        )
        outgoing = jnp.dot(send_map, terms, preferred_element_type=F32).astype(BF)
        outgoing = outgoing.reshape(peers, cap, tb, width)
        arrived = lax.all_to_all(
            outgoing, ("section", "tile"), split_axis=0, concat_axis=0, tiled=True
        )
        arrived = arrived.reshape(peers * cap, tb * width)
        incoming = jnp.dot(recv_map, arrived, preferred_element_type=F32).reshape(
            blocks, tb, width
        )
        gathered = (own + incoming).astype(BF).reshape(blocks * tb, width)
        inner = jax.nn.relu(jnp.dot(gathered, w_up[hop], preferred_element_type=F32)).astype(BF)
        state = state + jnp.dot(inner, w_down[hop], preferred_element_type=F32)
    return state.astype(BF)[None]


def solution(mesh):
    return jax.shard_map(
        local,
        mesh=mesh,
        in_specs=(
            P("slide", ("section", "tile"), None),
            P(("section", "tile", "slide"), None),
            P(),
            P(),
            P(),
            P("slide", ("section", "tile"), None, None),
            P("slide", ("section", "tile"), None, None, None),
            P("slide", None, None),
            P("slide", ("section", "tile")),
        ),
        out_specs=P("slide", ("section", "tile"), None),
        check_vma=False,
    )
```

```python
import functools

import jax
import jax.numpy as jnp
from jax import lax
from jax.experimental import pallas as pl
from jax.experimental.pallas import tpu as pltpu
from jax.sharding import PartitionSpec as P

MESH = pl.DeviceIdType.MESH
CORES = 2
PARTS = 2
BF = jnp.bfloat16
F32 = jnp.float32


def remote(src, dst, send_sem, recv_sem, device):
    return pltpu.make_async_remote_copy(
        src_ref=src,
        dst_ref=dst,
        send_sem=send_sem,
        recv_sem=recv_sem,
        device_id=device,
        device_id_type=MESH,
    )


def near_first(count):
    order = [0]
    for step in range(1, count // 2 + 1):
        order += [step] if step == count - step else [step, count - step]
    return order


def greet(devices):
    barrier = pltpu.get_barrier_semaphore()
    for device in devices:
        pl.semaphore_signal(barrier, inc=1, device_id=device, device_id_type=MESH)
    return lambda: pl.semaphore_wait(barrier, len(devices))


def encode_kernel(tiles, x_hbm, w_ref, fc_hbm, out_ref, x_ref, fc_ref, w_all, acc, ld, z_s, z_r, xy_s, xy_r, dg_s, dg_r, pt_s, pt_r):
    zs = tiles // CORES
    rows = w_ref.shape[0]
    half = rows // 2
    sx = lax.axis_index("section")
    sy = lax.axis_index("slide")
    t = lax.axis_index("tile")
    z, c = t // CORES, t % CORES
    ox, oy, oc = 1 - sx, 1 - sy, 1 - c
    partner = {"tile": z * CORES + oc}
    xn, yn = {"section": ox}, {"slide": oy}

    def zdev(o):
        return {"tile": ((z + o) % zs) * CORES + c}

    def at(x, o, core, y, part=None):
        zz = (z + o) % zs
        start = ((x * tiles + zz * CORES + core) * 2 + y) * rows
        if part is None:
            return w_all.at[pl.ds(pl.multiple_of(start, rows), rows)]
        return w_all.at[pl.ds(pl.multiple_of(start + part * half, half), half)]

    started = []

    def go(src, dst, ss, rs, device):
        copy = remote(src, dst, ss, rs, device)
        copy.start()
        started.append(copy)

    def arrived(dst, ss, rs, device):
        remote(dst, dst, ss, rs, device).wait_recv()

    loads = [pltpu.make_async_copy(x_hbm, x_ref, ld.at[0]), pltpu.make_async_copy(fc_hbm, fc_ref, ld.at[1])]
    for load in loads:
        load.start()
    wait = greet([partner, xn, yn] + [zdev(o) for o in range(1, zs)])
    start = ((sx * tiles + t) * 2 + sy) * rows
    w_all[pl.ds(pl.multiple_of(start, rows), rows)] = w_ref[...]
    wait()

    order = near_first(zs)
    for o in order[1:]:
        go(w_ref, at(sx, 0, c, sy), z_s.at[o], z_r.at[o], zdev(o))

    def line(o):
        src = w_ref if o == 0 else at(sx, o, c, sy)
        if o:
            arrived(src, z_s.at[0], z_r.at[zs - o], zdev(o))
        here = at(sx, o, c, sy)
        go(src, here, xy_s.at[0, o], xy_r.at[0, o], xn)
        go(src, here, xy_s.at[1, o], xy_r.at[1, o], yn)
        go(src, here, pt_s.at[0, o], pt_r.at[0, o], partner)

    def cross(o):
        ref = at(ox, o, c, sy)
        arrived(ref, xy_s.at[0, o], xy_r.at[0, o], xn)
        part = at(ox, o, c, sy, 0)
        go(part, part, dg_s.at[0, o], dg_r.at[0, o], yn)
        go(ref, ref, pt_s.at[1, o], pt_r.at[1, o], partner)
        ref = at(sx, o, c, oy)
        arrived(ref, xy_s.at[1, o], xy_r.at[1, o], yn)
        part = at(sx, o, c, oy, 1)
        go(part, part, dg_s.at[1, o], dg_r.at[1, o], xn)
        go(ref, ref, pt_s.at[2, o], pt_r.at[2, o], partner)

    def corner(o):
        for k, device in enumerate((yn, xn)):
            part = at(ox, o, c, oy, k)
            arrived(part, dg_s.at[k, o], dg_r.at[k, o], device)
            go(part, part, pt_s.at[3 + k, o], pt_r.at[3 + k, o], partner)

    depth = CORES * 2 * rows

    def multiply(o, first):
        refs = [at(sx, o, oc, sy), at(ox, o, oc, sy), at(sx, o, oc, oy), at(ox, o, oc, oy, 0), at(ox, o, oc, oy, 1)]
        for k, ref in enumerate(refs):
            arrived(ref, pt_s.at[k, o], pt_r.at[k, o], partner)
        cols = [((x * zs) + (z + o) % zs) * depth for x in (sx, ox)]
        slabs = [pl.ds(pl.multiple_of(s, depth), depth) for s in cols]
        tall = x_ref.shape[0] // 4

        def body(i, carry):
            strip = pl.ds(pl.multiple_of(i * tall, tall), tall)
            total = jnp.dot(x_ref[strip, slabs[0]], w_all[slabs[0], :], preferred_element_type=F32)
            total += jnp.dot(x_ref[strip, slabs[1]], w_all[slabs[1], :], preferred_element_type=F32)
            acc[strip, :] = total if first else acc[strip, :] + total
            return carry

        lax.fori_loop(0, 4, body, 0)

    for step in range(zs + 3):
        if step < zs:
            line(order[step])
        if 0 <= step - 1 < zs:
            cross(order[step - 1])
        if 0 <= step - 2 < zs:
            corner(order[step - 2])
        if step == 3:
            loads[0].wait()
        if 0 <= step - 3 < zs:
            multiply(order[step - 3], step == 3)

    tall = x_ref.shape[0] // 4
    loads[1].wait()

    def finish(i, carry):
        strip = pl.ds(pl.multiple_of(i * tall, tall), tall)
        enc = jnp.maximum(acc[strip, :], 0.0).astype(BF)
        out_ref[strip, :] = jnp.dot(enc, fc_ref[...], preferred_element_type=F32)
        return carry

    lax.fori_loop(0, 4, finish, 0)
    for copy in started:
        copy.wait_send()


def encode(rows, w_proj, w_fc):
    tiles = lax.axis_size("tile")
    zs = tiles // CORES
    vmem = pl.BlockSpec(memory_space=pltpu.VMEM)
    hbm = pl.BlockSpec(memory_space=pltpu.HBM)
    dma = pltpu.SemaphoreType.DMA
    return pl.pallas_call(
        functools.partial(encode_kernel, tiles),
        out_shape=jax.ShapeDtypeStruct((rows.shape[0], w_fc.shape[1]), F32),
        in_specs=[hbm, vmem, hbm],
        out_specs=vmem,
        scratch_shapes=[
            pltpu.VMEM(rows.shape, BF),
            pltpu.VMEM(w_fc.shape, BF),
            pltpu.VMEM((rows.shape[1], w_proj.shape[1]), BF),
            pltpu.VMEM((rows.shape[0], w_proj.shape[1]), F32),
            dma((2,)),
            dma((zs,)),
            dma((zs,)),
            dma((2, zs)),
            dma((2, zs)),
            dma((2, zs)),
            dma((2, zs)),
            dma((5, zs)),
            dma((5, zs)),
        ],
        compiler_params=pltpu.CompilerParams(
            collective_id=0, has_side_effects=True, vmem_limit_bytes=40 << 20
        ),
        name="encode",
    )(rows, w_proj, w_fc)


def hops_kernel(tiles, cap, parts, list_ref, state_ref, adj_ref, self_ref, up_ref, down_ref, out_ref,
                state, terms, send0, own0, recv0, send1, recv1, send2, recv2, send3, recv3, agg,
                s0, r0, s1, r1, s2, r2, s3, r3):
    hops = up_ref.shape[0]
    zs = tiles // CORES
    far = zs // 2
    blocks, slots, tb, _ = adj_ref.shape
    width = state_ref.shape[1]
    sends = blocks * slots
    per = blocks // parts
    chunks = zs * parts
    sx = lax.axis_index("section")
    t = lax.axis_index("tile")
    z, c = t // CORES, t % CORES
    ox, oc = 1 - sx, 1 - c
    oz = z + 1 - 2 * (z % 2)
    partner = {"tile": z * CORES + oc}
    xn = {"section": ox}
    zn = {"tile": oz * CORES + c}

    def zdev(j):
        return {"tile": ((z + 2 * j) % zs) * CORES + c}

    order = []
    for j in range(1, far):
        order += [(oz + 2 * j) % zs, (z + 2 * j) % zs]
    order += [oz, z]

    wait = greet([partner, xn, zn] + [zdev(j) for j in range(1, far)])
    terms[sends] = jnp.zeros((tb, width), BF)
    state[...] = state_ref[...]

    def term(b, carry):
        nodes = state[pl.ds(pl.multiple_of(b * tb, tb), tb), :].astype(BF)
        whole = jnp.dot(adj_ref[b].reshape(slots * tb, tb), nodes, preferred_element_type=F32)
        terms[pl.ds(b * slots, slots)] = whole.astype(BF).reshape(slots, tb, width)
        agg[pl.ds(pl.multiple_of(b * tb, tb), tb), :] = jnp.dot(self_ref[b], nodes, preferred_element_type=F32)
        return carry

    lax.fori_loop(0, blocks, term, 0)
    wait()

    for hop in range(hops):
        pending = []

        def go(src, dst, ss, rs, device):
            copy = remote(src, dst, ss, rs, device)
            copy.start()
            pending.append(copy)

        def arrived(dst, ss, rs, device):
            remote(dst, dst, ss, rs, device).wait_recv()

        def sums(dst, x, q, core):
            i, h = divmod(q, parts)
            first = ((x * zs + order[i]) * CORES + core) * blocks + h * per

            def body(r, carry):
                base = (first + r) * cap
                total = terms[list_ref[base]].astype(F32)
                for j in range(1, cap):
                    total += terms[list_ref[base + j]].astype(F32)
                dst[r] = total.astype(BF)
                return carry

            lax.fori_loop(0, per, body, 0)

        def chip(k, q):
            x = (ox, sx)[k]
            sums(send0.at[k, q], x, q, oc)
            go(send0.at[k, q], recv0.at[hop, k, q], s0.at[hop, k, q], r0.at[hop, k, q], partner)
            sums(own0.at[k, q], x, q, c)

        def pair(q):
            arrived(recv0.at[hop, 0, q], s0.at[hop, 0, q], r0.at[hop, 0, q], partner)

            def body(r, carry):
                send1[q, r] = (own0[0, q, r].astype(F32) + recv0[hop, 0, q, r].astype(F32)).astype(BF)
                return carry

            lax.fori_loop(0, per, body, 0)
            go(send1.at[q], recv1.at[hop, q], s1.at[hop, q], r1.at[hop, q], xn)

        chip(0, 0)
        for q in range(1, chunks):
            chip(0, q)
            pair(q - 1)
        chip(1, 0)
        pair(chunks - 1)
        for q in range(1, chunks):
            chip(1, q)

        for q in range(chunks):
            i, h = divmod(q, parts)
            arrived(recv0.at[hop, 1, q], s0.at[hop, 1, q], r0.at[hop, 1, q], partner)
            arrived(recv1.at[hop, q], s1.at[hop, q], r1.at[hop, q], xn)
            slot = (i // 2) * parts + h
            onward = i % 2 == 0
            if not onward:
                arrived(recv2.at[hop, slot], s2.at[hop, slot], r2.at[hop, slot], zn)
            home = i == zs - 1

            def gathered(r):
                total = own0[1, q, r].astype(F32) + recv0[hop, 1, q, r].astype(F32)
                total += recv1[hop, q, r].astype(F32)
                return total if onward else total + recv2[hop, slot, r].astype(F32)

            if not home:
                out = send2 if onward else send3

                def body(r, carry):
                    out[slot, r] = gathered(r).astype(BF)
                    return carry

                lax.fori_loop(0, per, body, 0)
                if onward:
                    go(send2.at[slot], recv2.at[hop, slot], s2.at[hop, slot], r2.at[hop, slot], zn)
                else:
                    go(send3.at[slot], recv3.at[hop, slot], s3.at[hop, slot], r3.at[hop, slot], zdev(i // 2 + 1))
                continue
            for j in range(1, far):
                there = (j - 1) * parts + h
                arrived(recv3.at[hop, there], s3.at[hop, there], r3.at[hop, there], zdev(j))

            def finish(r, carry):
                rows = pl.ds(pl.multiple_of((h * per + r) * tb, tb), tb)
                total = agg[rows, :] + gathered(r)
                for j in range(1, far):
                    total += recv3[hop, (j - 1) * parts + h, r].astype(F32)
                inner = jnp.dot(total.astype(BF), up_ref[hop], preferred_element_type=F32)
                inner = jnp.maximum(inner, 0.0).astype(BF)
                after = state[rows, :] + jnp.dot(inner, down_ref[hop], preferred_element_type=F32)
                if hop == hops - 1:
                    out_ref[rows, :] = after.astype(BF)
                else:
                    state[rows, :] = after
                return carry

            lax.fori_loop(0, per, finish, 0, unroll=True)
            if hop < hops - 1:
                lax.fori_loop(h * per, h * per + per, term, 0)
        for copy in pending:
            copy.wait_send()


def graph(state, adjacency, self_adj, w_up, w_down, lists, cap):
    tiles = lax.axis_size("tile")
    zs = tiles // CORES
    far = zs // 2
    blocks, slots, tb, _ = adjacency.shape
    width = state.shape[1]
    hops = w_up.shape[0]
    parts = PARTS if blocks % PARTS == 0 else 1
    piece = (blocks // parts, tb, width)
    chunks = zs * parts
    onward = far * parts
    distant = max(1, (far - 1) * parts)
    vmem = pl.BlockSpec(memory_space=pltpu.VMEM)
    dma = pltpu.SemaphoreType.DMA
    return pl.pallas_call(
        functools.partial(hops_kernel, tiles, cap, parts),
        out_shape=jax.ShapeDtypeStruct(state.shape, BF),
        in_specs=[pl.BlockSpec(memory_space=pltpu.SMEM)] + [vmem] * 5,
        out_specs=vmem,
        scratch_shapes=[
            pltpu.VMEM(state.shape, F32),
            pltpu.VMEM((blocks * slots + 1, tb, width), BF),
            pltpu.VMEM((2, chunks) + piece, BF),
            pltpu.VMEM((2, chunks) + piece, BF),
            pltpu.VMEM((hops, 2, chunks) + piece, BF),
            pltpu.VMEM((chunks,) + piece, BF),
            pltpu.VMEM((hops, chunks) + piece, BF),
            pltpu.VMEM((onward,) + piece, BF),
            pltpu.VMEM((hops, onward) + piece, BF),
            pltpu.VMEM((distant,) + piece, BF),
            pltpu.VMEM((hops, distant) + piece, BF),
            pltpu.VMEM(state.shape, F32),
        ]
        + [dma((hops, 2, chunks))] * 2
        + [dma((hops, chunks))] * 2
        + [dma((hops, onward))] * 2
        + [dma((hops, distant))] * 2,
        compiler_params=pltpu.CompilerParams(
            collective_id=1, has_side_effects=True, vmem_limit_bytes=50 << 20
        ),
        name="hops",
    )(lists, state, adjacency, self_adj, w_up, w_down)


def entry_lists(targets, live, total_blocks, cap):
    sends = targets.shape[0]
    positions = jnp.arange(sends, dtype=jnp.int32)
    same = (targets[:, None] == targets[None, :]) & live[None, :] & (positions[None, :] < positions[:, None])
    rank = jnp.sum(same.astype(jnp.int32), axis=1)
    hit = (jnp.arange(total_blocks, dtype=jnp.int32)[:, None, None] == targets[None, None, :]) & live[None, None, :]
    hit = hit & (jnp.arange(cap, dtype=jnp.int32)[None, :, None] == rank[None, None, :])
    found = jnp.sum(jnp.where(hit, positions[None, None, :] - sends, 0), axis=2) + sends
    return found.reshape(total_blocks * cap)


def local(features, w_proj, w_fc, w_up, w_down, self_adj, adjacency, nbr_block, counts):
    rows = features[0]
    blocks = self_adj.shape[1]
    tb = self_adj.shape[2]
    width = w_fc.shape[1]
    slots = adjacency.shape[2]
    hops = w_up.shape[0]
    pairs = lax.axis_size("section") == 2 and lax.axis_size("tile") % (2 * CORES) == 0
    peers = lax.axis_size("section") * lax.axis_size("tile")
    me_index = lax.axis_index("section") * lax.axis_size("tile") + lax.axis_index("tile")
    sends = blocks * slots
    cap = (sends + peers - 1) // peers
    if pairs and lax.axis_size("slide") == 2 and w_proj.shape[0] % 32 == 0:
        state = encode(rows, w_proj, w_fc)
    else:
        pre = jnp.dot(
            rows,
            lax.all_gather(w_proj, ("section", "tile", "slide"), axis=0, tiled=True),
            preferred_element_type=F32,
        )
        encoded = jax.nn.relu(pre).astype(BF)
        state = jnp.dot(encoded, w_fc, preferred_element_type=F32)
    live = jnp.arange(slots, dtype=jnp.int32)[None, :] < counts[0][:, None]
    if pairs and blocks <= CORES * cap:
        targets = lax.dynamic_slice_in_dim(nbr_block[0], me_index * blocks, blocks, 0).reshape(sends)
        lists = entry_lists(targets, live.reshape(sends), peers * blocks, cap)
        return graph(state, adjacency[0], self_adj[0], w_up, w_down, lists, cap)[None]
    table = nbr_block[0].reshape(peers, sends)
    target_dev = table // blocks
    target_local = table % blocks
    positions = jnp.arange(sends, dtype=jnp.int32)
    before = positions[None, :] < positions[:, None]
    same = target_dev[:, :, None] == target_dev[:, None, :]
    ranking = jnp.sum(jnp.logical_and(same, before[None]).astype(jnp.int32), axis=2)
    mine_dev = lax.dynamic_index_in_dim(target_dev, me_index, 0, keepdims=False)
    mine_rank = lax.dynamic_index_in_dim(ranking, me_index, 0, keepdims=False)
    slot_of = mine_dev * cap + mine_rank
    send_map = (jnp.arange(peers * cap, dtype=jnp.int32)[:, None] == slot_of[None, :]).astype(BF)
    arrive_hit = target_dev == me_index
    slot_flags = jnp.logical_and(
        arrive_hit[:, :, None],
        ranking[:, :, None] == jnp.arange(cap, dtype=jnp.int32)[None, None, :],
    ).astype(F32)
    local_flags = (
        target_local[:, :, None] == jnp.arange(blocks, dtype=jnp.int32)[None, None, :]
    ).astype(F32)
    recv_map = (
        jnp.einsum("pjc,pjr->rpc", slot_flags, local_flags).reshape(blocks, peers * cap).astype(BF)
    )
    for hop in range(hops):
        nodes = state.astype(BF).reshape(blocks, tb, width)
        own = jnp.einsum("bij,bjh->bih", self_adj[0], nodes, preferred_element_type=F32)
        terms = jnp.einsum("bkij,bjh->bkih", adjacency[0], nodes, preferred_element_type=F32)
        terms = (
            jnp.where(live[:, :, None, None], terms, 0.0).astype(BF).reshape(sends, tb * width)
        )
        outgoing = jnp.dot(send_map, terms, preferred_element_type=F32).astype(BF)
        outgoing = outgoing.reshape(peers, cap, tb, width)
        arrived = lax.all_to_all(
            outgoing, ("section", "tile"), split_axis=0, concat_axis=0, tiled=True
        )
        arrived = arrived.reshape(peers * cap, tb * width)
        incoming = jnp.dot(recv_map, arrived, preferred_element_type=F32).reshape(
            blocks, tb, width
        )
        gathered = (own + incoming).astype(BF).reshape(blocks * tb, width)
        inner = jax.nn.relu(jnp.dot(gathered, w_up[hop], preferred_element_type=F32)).astype(BF)
        state = state + jnp.dot(inner, w_down[hop], preferred_element_type=F32)
    return state.astype(BF)[None]


def solution(mesh):
    return jax.shard_map(
        local,
        mesh=mesh,
        in_specs=(
            P("slide", ("section", "tile"), None),
            P(("section", "tile", "slide"), None),
            P(),
            P(),
            P(),
            P("slide", ("section", "tile"), None, None),
            P("slide", ("section", "tile"), None, None, None),
            P("slide", None, None),
            P("slide", ("section", "tile")),
        ),
        out_specs=P("slide", ("section", "tile"), None),
        check_vma=False,
    )
```

```python
import functools

import jax
import jax.numpy as jnp
from jax import lax
from jax.experimental import pallas as pl
from jax.experimental.pallas import tpu as pltpu
from jax.sharding import PartitionSpec as P

MESH = pl.DeviceIdType.MESH
CORES = 2
PARTS = 2
BF = jnp.bfloat16
F32 = jnp.float32


def remote(src, dst, send_sem, recv_sem, device):
    return pltpu.make_async_remote_copy(
        src_ref=src,
        dst_ref=dst,
        send_sem=send_sem,
        recv_sem=recv_sem,
        device_id=device,
        device_id_type=MESH,
    )


def greet(devices):
    barrier = pltpu.get_barrier_semaphore()
    for device in devices:
        pl.semaphore_signal(barrier, inc=1, device_id=device, device_id_type=MESH)
    return lambda: pl.semaphore_wait(barrier, len(devices))


def encode_kernel(tiles, x_hbm, w_ref, fc_hbm, out_ref, x_ref, fc_ref, w_all, acc, ld, z_s, z_r, xy_s, xy_r, dg_s, dg_r, pt_s, pt_r):
    zs = tiles // CORES
    far = zs // 2
    rows = w_ref.shape[0]
    half = rows // 2
    sx = lax.axis_index("section")
    sy = lax.axis_index("slide")
    t = lax.axis_index("tile")
    z, c = t // CORES, t % CORES
    ox, oy, oc = 1 - sx, 1 - sy, 1 - c
    oz = z + 1 - 2 * (z % 2)
    partner = {"tile": z * CORES + oc}
    xn, yn, zn = {"section": ox}, {"slide": oy}, {"tile": oz * CORES + c}
    places = [z] + [(z + 2 * j) % zs for j in range(1, far)] + [oz] + [(oz + 2 * j) % zs for j in range(1, far)]

    def zdev(j):
        return {"tile": ((z + 2 * j) % zs) * CORES + c}

    def at(x, m, core, y, k):
        start = ((x * tiles + places[m] * CORES + core) * 2 + y) * rows + k * half
        return w_all.at[pl.ds(pl.multiple_of(start, half), half)]

    started = []

    def go(src, dst, ss, rs, device):
        copy = remote(src, dst, ss, rs, device)
        copy.start()
        started.append(copy)

    def arrived(dst, ss, rs, device):
        remote(dst, dst, ss, rs, device).wait_recv()

    loads = [pltpu.make_async_copy(x_hbm, x_ref, ld.at[0]), pltpu.make_async_copy(fc_hbm, fc_ref, ld.at[1])]
    wait = greet([partner, xn, yn, zn] + [zdev(j) for j in range(1, far)])
    for load in loads:
        load.start()
    start = ((sx * tiles + t) * 2 + sy) * rows
    w_all[pl.ds(pl.multiple_of(start, rows), rows)] = w_ref[...]
    wait()

    def own(k):
        return w_ref.at[pl.ds(k * half, half)]

    for k in range(2):
        for j in range(1, far):
            go(own(k), at(sx, 0, c, sy, k), z_s.at[j, k], z_r.at[j, k], zdev(j))
    for k in range(2):
        go(own(k), at(sx, 0, c, sy, k), z_s.at[far, k], z_r.at[far, k], zn)

    def line(m, k):
        here = at(sx, m, c, sy, k)
        src = here if m else own(k)
        if 0 < m < far:
            arrived(here, z_s.at[0, k], z_r.at[far - m, k], zdev(m))
        elif m:
            arrived(here, z_s.at[0, k], z_r.at[m, k], zn)
        go(src, here, xy_s.at[0, m, k], xy_r.at[0, m, k], xn)
        go(src, here, xy_s.at[1, m, k], xy_r.at[1, m, k], yn)
        if 0 < m < far:
            go(src, here, z_s.at[far + m, k], z_r.at[far + m, k], zn)
        go(src, here, pt_s.at[0, m, k], pt_r.at[0, m, k], partner)

    def cross(m, k):
        for kind, device, other, ref in (
            (0, xn, yn, at(ox, m, c, sy, k)),
            (1, yn, xn, at(sx, m, c, oy, k)),
        ):
            arrived(ref, xy_s.at[kind, m, k], xy_r.at[kind, m, k], device)
            if k == kind:
                go(ref, ref, dg_s.at[m, k], dg_r.at[m, k], other)
            go(ref, ref, pt_s.at[1 + kind, m, k], pt_r.at[1 + kind, m, k], partner)

    def corner(m, k):
        ref = at(ox, m, c, oy, k)
        arrived(ref, dg_s.at[m, k], dg_r.at[m, k], (yn, xn)[k])
        go(ref, ref, pt_s.at[3, m, k], pt_r.at[3, m, k], partner)

    depth = CORES * 2 * rows
    tall = x_ref.shape[0] // 4

    def multiply(m):
        for k in range(2):
            for kind, (x, y) in enumerate(((sx, sy), (ox, sy), (sx, oy), (ox, oy))):
                arrived(at(x, m, oc, y, k), pt_s.at[kind, m, k], pt_r.at[kind, m, k], partner)
        slabs = [pl.ds(pl.multiple_of((x * zs + places[m]) * depth, depth), depth) for x in (sx, ox)]

        def body(i, carry):
            strip = pl.ds(pl.multiple_of(i * tall, tall), tall)
            total = jnp.dot(x_ref[strip, slabs[0]], w_all[slabs[0], :], preferred_element_type=F32)
            total += jnp.dot(x_ref[strip, slabs[1]], w_all[slabs[1], :], preferred_element_type=F32)
            if m:
                total += acc[strip, :]
            if m < zs - 1:
                acc[strip, :] = total
            else:
                enc = jnp.maximum(total, 0.0).astype(BF)
                out_ref[strip, :] = jnp.dot(enc, fc_ref[...], preferred_element_type=F32)
            return carry

        lax.fori_loop(0, 4, body, 0)

    steps = [(m, k) for m in range(zs) for k in range(2)]
    count = len(steps)
    for step in range(count + 5):
        if step < count:
            line(*steps[step])
        if 0 <= step - 2 < count:
            cross(*steps[step - 2])
        if 0 <= step - 4 < count:
            corner(*steps[step - 4])
        if step == 5:
            for load in loads:
                load.wait()
        if 0 <= step - 5 < count and steps[step - 5][1]:
            multiply(steps[step - 5][0])
    for copy in started:
        copy.wait_send()


def encode(rows, w_proj, w_fc):
    tiles = lax.axis_size("tile")
    zs = tiles // CORES
    vmem = pl.BlockSpec(memory_space=pltpu.VMEM)
    hbm = pl.BlockSpec(memory_space=pltpu.HBM)
    dma = pltpu.SemaphoreType.DMA
    return pl.pallas_call(
        functools.partial(encode_kernel, tiles),
        out_shape=jax.ShapeDtypeStruct((rows.shape[0], w_fc.shape[1]), F32),
        in_specs=[hbm, vmem, hbm],
        out_specs=vmem,
        scratch_shapes=[
            pltpu.VMEM(rows.shape, BF),
            pltpu.VMEM(w_fc.shape, BF),
            pltpu.VMEM((rows.shape[1], w_proj.shape[1]), BF),
            pltpu.VMEM((rows.shape[0], w_proj.shape[1]), F32),
            dma((2,)),
            dma((zs, 2)),
            dma((zs, 2)),
            dma((2, zs, 2)),
            dma((2, zs, 2)),
            dma((zs, 2)),
            dma((zs, 2)),
            dma((4, zs, 2)),
            dma((4, zs, 2)),
        ],
        compiler_params=pltpu.CompilerParams(
            collective_id=0, has_side_effects=True, vmem_limit_bytes=61 << 20
        ),
        name="encode",
    )(rows, w_proj, w_fc)


def hops_kernel(tiles, cap, parts, list_ref, state_ref, adj_ref, self_ref, up_ref, down_ref, out_ref,
                state, terms, send0, own0, recv0, send1, recv1, send2, recv2, send3, recv3, agg,
                s0, r0, s1, r1, s2, r2, s3, r3):
    hops = up_ref.shape[0]
    zs = tiles // CORES
    far = zs // 2
    blocks, slots, tb, _ = adj_ref.shape
    width = state_ref.shape[1]
    sends = blocks * slots
    per = blocks // parts
    chunks = zs * parts
    sx = lax.axis_index("section")
    t = lax.axis_index("tile")
    z, c = t // CORES, t % CORES
    ox, oc = 1 - sx, 1 - c
    oz = z + 1 - 2 * (z % 2)
    partner = {"tile": z * CORES + oc}
    xn = {"section": ox}
    zn = {"tile": oz * CORES + c}

    def zdev(j):
        return {"tile": ((z + 2 * j) % zs) * CORES + c}

    order = []
    for j in range(1, far):
        order += [(oz + 2 * j) % zs, (z + 2 * j) % zs]
    order += [oz, z]

    wait = greet([partner, xn, zn] + [zdev(j) for j in range(1, far)])
    terms[sends] = jnp.zeros((tb, width), BF)
    state[...] = state_ref[...]

    def term(b, carry):
        nodes = state[pl.ds(pl.multiple_of(b * tb, tb), tb), :].astype(BF)
        whole = jnp.dot(adj_ref[b].reshape(slots * tb, tb), nodes, preferred_element_type=F32)
        terms[pl.ds(b * slots, slots)] = whole.astype(BF).reshape(slots, tb, width)
        agg[pl.ds(pl.multiple_of(b * tb, tb), tb), :] = jnp.dot(self_ref[b], nodes, preferred_element_type=F32)
        return carry

    lax.fori_loop(0, blocks, term, 0)
    wait()

    for hop in range(hops):
        pending = []

        def go(src, dst, ss, rs, device):
            copy = remote(src, dst, ss, rs, device)
            copy.start()
            pending.append(copy)

        def arrived(dst, ss, rs, device):
            remote(dst, dst, ss, rs, device).wait_recv()

        def sums(dst, x, q, core):
            i, h = divmod(q, parts)
            first = ((x * zs + order[i]) * CORES + core) * blocks + h * per

            def body(r, carry):
                base = (first + r) * cap
                total = terms[list_ref[base]].astype(F32)
                for j in range(1, cap):
                    total += terms[list_ref[base + j]].astype(F32)
                dst[r] = total.astype(BF)
                return carry

            lax.fori_loop(0, per, body, 0)

        def chip(k, q):
            x = (ox, sx)[k]
            sums(send0.at[k, q], x, q, oc)
            go(send0.at[k, q], recv0.at[hop, k, q], s0.at[hop, k, q], r0.at[hop, k, q], partner)
            sums(own0.at[k, q], x, q, c)

        def pair(q):
            arrived(recv0.at[hop, 0, q], s0.at[hop, 0, q], r0.at[hop, 0, q], partner)

            def body(r, carry):
                send1[q, r] = (own0[0, q, r].astype(F32) + recv0[hop, 0, q, r].astype(F32)).astype(BF)
                return carry

            lax.fori_loop(0, per, body, 0)
            go(send1.at[q], recv1.at[hop, q], s1.at[hop, q], r1.at[hop, q], xn)

        chip(0, 0)
        for q in range(1, chunks):
            chip(0, q)
            pair(q - 1)
        chip(1, 0)
        pair(chunks - 1)
        for q in range(1, chunks):
            chip(1, q)

        for q in range(chunks):
            i, h = divmod(q, parts)
            arrived(recv0.at[hop, 1, q], s0.at[hop, 1, q], r0.at[hop, 1, q], partner)
            arrived(recv1.at[hop, q], s1.at[hop, q], r1.at[hop, q], xn)
            slot = (i // 2) * parts + h
            onward = i % 2 == 0
            if not onward:
                arrived(recv2.at[hop, slot], s2.at[hop, slot], r2.at[hop, slot], zn)
            home = i == zs - 1

            def gathered(r):
                total = own0[1, q, r].astype(F32) + recv0[hop, 1, q, r].astype(F32)
                total += recv1[hop, q, r].astype(F32)
                return total if onward else total + recv2[hop, slot, r].astype(F32)

            if not home:
                out = send2 if onward else send3

                def body(r, carry):
                    out[slot, r] = gathered(r).astype(BF)
                    return carry

                lax.fori_loop(0, per, body, 0)
                if onward:
                    go(send2.at[slot], recv2.at[hop, slot], s2.at[hop, slot], r2.at[hop, slot], zn)
                else:
                    go(send3.at[slot], recv3.at[hop, slot], s3.at[hop, slot], r3.at[hop, slot], zdev(i // 2 + 1))
                continue
            for j in range(1, far):
                there = (j - 1) * parts + h
                arrived(recv3.at[hop, there], s3.at[hop, there], r3.at[hop, there], zdev(j))

            def finish(r, carry):
                rows = pl.ds(pl.multiple_of((h * per + r) * tb, tb), tb)
                total = agg[rows, :] + gathered(r)
                for j in range(1, far):
                    total += recv3[hop, (j - 1) * parts + h, r].astype(F32)
                inner = jnp.dot(total.astype(BF), up_ref[hop], preferred_element_type=F32)
                inner = jnp.maximum(inner, 0.0).astype(BF)
                after = state[rows, :] + jnp.dot(inner, down_ref[hop], preferred_element_type=F32)
                if hop == hops - 1:
                    out_ref[rows, :] = after.astype(BF)
                else:
                    state[rows, :] = after
                return carry

            lax.fori_loop(0, per, finish, 0, unroll=True)
            if hop < hops - 1:
                lax.fori_loop(h * per, h * per + per, term, 0)
        for copy in pending:
            copy.wait_send()


def graph(state, adjacency, self_adj, w_up, w_down, lists, cap):
    tiles = lax.axis_size("tile")
    zs = tiles // CORES
    far = zs // 2
    blocks, slots, tb, _ = adjacency.shape
    width = state.shape[1]
    hops = w_up.shape[0]
    parts = PARTS if blocks % PARTS == 0 else 1
    piece = (blocks // parts, tb, width)
    chunks = zs * parts
    onward = far * parts
    distant = max(1, (far - 1) * parts)
    vmem = pl.BlockSpec(memory_space=pltpu.VMEM)
    dma = pltpu.SemaphoreType.DMA
    return pl.pallas_call(
        functools.partial(hops_kernel, tiles, cap, parts),
        out_shape=jax.ShapeDtypeStruct(state.shape, BF),
        in_specs=[pl.BlockSpec(memory_space=pltpu.SMEM)] + [vmem] * 5,
        out_specs=vmem,
        scratch_shapes=[
            pltpu.VMEM(state.shape, F32),
            pltpu.VMEM((blocks * slots + 1, tb, width), BF),
            pltpu.VMEM((2, chunks) + piece, BF),
            pltpu.VMEM((2, chunks) + piece, BF),
            pltpu.VMEM((hops, 2, chunks) + piece, BF),
            pltpu.VMEM((chunks,) + piece, BF),
            pltpu.VMEM((hops, chunks) + piece, BF),
            pltpu.VMEM((onward,) + piece, BF),
            pltpu.VMEM((hops, onward) + piece, BF),
            pltpu.VMEM((distant,) + piece, BF),
            pltpu.VMEM((hops, distant) + piece, BF),
            pltpu.VMEM(state.shape, F32),
        ]
        + [dma((hops, 2, chunks))] * 2
        + [dma((hops, chunks))] * 2
        + [dma((hops, onward))] * 2
        + [dma((hops, distant))] * 2,
        compiler_params=pltpu.CompilerParams(
            collective_id=1, has_side_effects=True, vmem_limit_bytes=50 << 20
        ),
        name="hops",
    )(lists, state, adjacency, self_adj, w_up, w_down)


def entry_lists(targets, live, total_blocks, cap):
    sends = targets.shape[0]
    positions = jnp.arange(sends, dtype=jnp.int32)
    same = (targets[:, None] == targets[None, :]) & live[None, :] & (positions[None, :] < positions[:, None])
    rank = jnp.sum(same.astype(jnp.int32), axis=1)
    hit = (jnp.arange(total_blocks, dtype=jnp.int32)[:, None, None] == targets[None, None, :]) & live[None, None, :]
    hit = hit & (jnp.arange(cap, dtype=jnp.int32)[None, :, None] == rank[None, None, :])
    found = jnp.sum(jnp.where(hit, positions[None, None, :] - sends, 0), axis=2) + sends
    return found.reshape(total_blocks * cap)


def local(features, w_proj, w_fc, w_up, w_down, self_adj, adjacency, nbr_block, counts):
    rows = features[0]
    blocks = self_adj.shape[1]
    tb = self_adj.shape[2]
    width = w_fc.shape[1]
    slots = adjacency.shape[2]
    hops = w_up.shape[0]
    pairs = lax.axis_size("section") == 2 and lax.axis_size("tile") % (2 * CORES) == 0
    peers = lax.axis_size("section") * lax.axis_size("tile")
    me_index = lax.axis_index("section") * lax.axis_size("tile") + lax.axis_index("tile")
    sends = blocks * slots
    cap = (sends + peers - 1) // peers
    if pairs and lax.axis_size("slide") == 2 and w_proj.shape[0] % 32 == 0:
        state = encode(rows, w_proj, w_fc)
    else:
        pre = jnp.dot(
            rows,
            lax.all_gather(w_proj, ("section", "tile", "slide"), axis=0, tiled=True),
            preferred_element_type=F32,
        )
        encoded = jax.nn.relu(pre).astype(BF)
        state = jnp.dot(encoded, w_fc, preferred_element_type=F32)
    live = jnp.arange(slots, dtype=jnp.int32)[None, :] < counts[0][:, None]
    if pairs and blocks <= CORES * cap:
        targets = lax.dynamic_slice_in_dim(nbr_block[0], me_index * blocks, blocks, 0).reshape(sends)
        lists = entry_lists(targets, live.reshape(sends), peers * blocks, cap)
        return graph(state, adjacency[0], self_adj[0], w_up, w_down, lists, cap)[None]
    table = nbr_block[0].reshape(peers, sends)
    target_dev = table // blocks
    target_local = table % blocks
    positions = jnp.arange(sends, dtype=jnp.int32)
    before = positions[None, :] < positions[:, None]
    same = target_dev[:, :, None] == target_dev[:, None, :]
    ranking = jnp.sum(jnp.logical_and(same, before[None]).astype(jnp.int32), axis=2)
    mine_dev = lax.dynamic_index_in_dim(target_dev, me_index, 0, keepdims=False)
    mine_rank = lax.dynamic_index_in_dim(ranking, me_index, 0, keepdims=False)
    slot_of = mine_dev * cap + mine_rank
    send_map = (jnp.arange(peers * cap, dtype=jnp.int32)[:, None] == slot_of[None, :]).astype(BF)
    arrive_hit = target_dev == me_index
    slot_flags = jnp.logical_and(
        arrive_hit[:, :, None],
        ranking[:, :, None] == jnp.arange(cap, dtype=jnp.int32)[None, None, :],
    ).astype(F32)
    local_flags = (
        target_local[:, :, None] == jnp.arange(blocks, dtype=jnp.int32)[None, None, :]
    ).astype(F32)
    recv_map = (
        jnp.einsum("pjc,pjr->rpc", slot_flags, local_flags).reshape(blocks, peers * cap).astype(BF)
    )
    for hop in range(hops):
        nodes = state.astype(BF).reshape(blocks, tb, width)
        own = jnp.einsum("bij,bjh->bih", self_adj[0], nodes, preferred_element_type=F32)
        terms = jnp.einsum("bkij,bjh->bkih", adjacency[0], nodes, preferred_element_type=F32)
        terms = (
            jnp.where(live[:, :, None, None], terms, 0.0).astype(BF).reshape(sends, tb * width)
        )
        outgoing = jnp.dot(send_map, terms, preferred_element_type=F32).astype(BF)
        outgoing = outgoing.reshape(peers, cap, tb, width)
        arrived = lax.all_to_all(
            outgoing, ("section", "tile"), split_axis=0, concat_axis=0, tiled=True
        )
        arrived = arrived.reshape(peers * cap, tb * width)
        incoming = jnp.dot(recv_map, arrived, preferred_element_type=F32).reshape(
            blocks, tb, width
        )
        gathered = (own + incoming).astype(BF).reshape(blocks * tb, width)
        inner = jax.nn.relu(jnp.dot(gathered, w_up[hop], preferred_element_type=F32)).astype(BF)
        state = state + jnp.dot(inner, w_down[hop], preferred_element_type=F32)
    return state.astype(BF)[None]


def solution(mesh):
    return jax.shard_map(
        local,
        mesh=mesh,
        in_specs=(
            P("slide", ("section", "tile"), None),
            P(("section", "tile", "slide"), None),
            P(),
            P(),
            P(),
            P("slide", ("section", "tile"), None, None),
            P("slide", ("section", "tile"), None, None, None),
            P("slide", None, None),
            P("slide", ("section", "tile")),
        ),
        out_specs=P("slide", ("section", "tile"), None),
        check_vma=False,
    )
```

```python
import functools

import jax
import jax.numpy as jnp
from jax import lax
from jax.experimental import pallas as pl
from jax.experimental.pallas import tpu as pltpu
from jax.sharding import PartitionSpec as P

MESH = pl.DeviceIdType.MESH
CORES = 2
PARTS = 2
BF = jnp.bfloat16
F32 = jnp.float32


def remote(src, dst, send_sem, recv_sem, device):
    return pltpu.make_async_remote_copy(
        src_ref=src,
        dst_ref=dst,
        send_sem=send_sem,
        recv_sem=recv_sem,
        device_id=device,
        device_id_type=MESH,
    )


def greet(devices):
    barrier = pltpu.get_barrier_semaphore()
    for device in devices:
        pl.semaphore_signal(barrier, inc=1, device_id=device, device_id_type=MESH)
    return lambda: pl.semaphore_wait(barrier, len(devices))


def encode_kernel(tiles, x_hbm, w_ref, fc_hbm, out_ref, x_ref, fc_ref, w_all, acc, ld, z_s, z_r, xy_s, xy_r, dg_s, dg_r, pt_s, pt_r):
    zs = tiles // CORES
    far = zs // 2
    rows = w_ref.shape[0]
    half = rows // 2
    sx = lax.axis_index("section")
    sy = lax.axis_index("slide")
    t = lax.axis_index("tile")
    z, c = t // CORES, t % CORES
    ox, oy, oc = 1 - sx, 1 - sy, 1 - c
    oz = z + 1 - 2 * (z % 2)
    partner = {"tile": z * CORES + oc}
    xn, yn, zn = {"section": ox}, {"slide": oy}, {"tile": oz * CORES + c}
    places = [z] + [(z + 2 * j) % zs for j in range(1, far)] + [oz] + [(oz + 2 * j) % zs for j in range(1, far)]

    def zdev(j):
        return {"tile": ((z + 2 * j) % zs) * CORES + c}

    def at(x, m, core, y, k):
        start = ((x * tiles + places[m] * CORES + core) * 2 + y) * rows + k * half
        return w_all.at[pl.ds(pl.multiple_of(start, half), half)]

    started = []

    def go(src, dst, ss, rs, device):
        copy = remote(src, dst, ss, rs, device)
        copy.start()
        started.append(copy)

    def arrived(dst, ss, rs, device):
        remote(dst, dst, ss, rs, device).wait_recv()

    loads = [pltpu.make_async_copy(x_hbm, x_ref, ld.at[0]), pltpu.make_async_copy(fc_hbm, fc_ref, ld.at[1])]
    wait = greet([partner, xn, yn, zn] + [zdev(j) for j in range(1, far)])
    for load in loads:
        load.start()
    start = ((sx * tiles + t) * 2 + sy) * rows
    w_all[pl.ds(pl.multiple_of(start, rows), rows)] = w_ref[...]
    wait()

    def own(k):
        return w_ref.at[pl.ds(k * half, half)]

    for k in range(2):
        for j in range(1, far):
            go(own(k), at(sx, 0, c, sy, k), z_s.at[j, k], z_r.at[j, k], zdev(j))
    for k in range(2):
        go(own(k), at(sx, 0, c, sy, k), z_s.at[far, k], z_r.at[far, k], zn)

    def line(m, k):
        here = at(sx, m, c, sy, k)
        src = here if m else own(k)
        if 0 < m < far:
            arrived(here, z_s.at[0, k], z_r.at[far - m, k], zdev(m))
        elif m:
            arrived(here, z_s.at[0, k], z_r.at[m, k], zn)
        go(src, here, xy_s.at[0, m, k], xy_r.at[0, m, k], xn)
        go(src, here, xy_s.at[1, m, k], xy_r.at[1, m, k], yn)
        if 0 < m < far:
            go(src, here, z_s.at[far + m, k], z_r.at[far + m, k], zn)
        go(src, here, pt_s.at[0, m, k], pt_r.at[0, m, k], partner)

    def cross(m, k):
        for kind, device, other, ref in (
            (0, xn, yn, at(ox, m, c, sy, k)),
            (1, yn, xn, at(sx, m, c, oy, k)),
        ):
            arrived(ref, xy_s.at[kind, m, k], xy_r.at[kind, m, k], device)
            if k == kind:
                go(ref, ref, dg_s.at[m, k], dg_r.at[m, k], other)
            go(ref, ref, pt_s.at[1 + kind, m, k], pt_r.at[1 + kind, m, k], partner)

    def corner(m, k):
        ref = at(ox, m, c, oy, k)
        arrived(ref, dg_s.at[m, k], dg_r.at[m, k], (yn, xn)[k])
        go(ref, ref, pt_s.at[3, m, k], pt_r.at[3, m, k], partner)

    depth = CORES * 2 * rows
    tall = x_ref.shape[0] // 4

    def multiply(m):
        for k in range(2):
            for kind, (x, y) in enumerate(((sx, sy), (ox, sy), (sx, oy), (ox, oy))):
                arrived(at(x, m, oc, y, k), pt_s.at[kind, m, k], pt_r.at[kind, m, k], partner)
        slabs = [pl.ds(pl.multiple_of((x * zs + places[m]) * depth, depth), depth) for x in (sx, ox)]

        def body(i, carry):
            strip = pl.ds(pl.multiple_of(i * tall, tall), tall)
            total = jnp.dot(x_ref[strip, slabs[0]], w_all[slabs[0], :], preferred_element_type=F32)
            total += jnp.dot(x_ref[strip, slabs[1]], w_all[slabs[1], :], preferred_element_type=F32)
            if m:
                total += acc[strip, :]
            if m < zs - 1:
                acc[strip, :] = total
            else:
                enc = jnp.maximum(total, 0.0).astype(BF)
                out_ref[strip, :] = jnp.dot(enc, fc_ref[...], preferred_element_type=F32)
            return carry

        lax.fori_loop(0, 4, body, 0)

    steps = [(m, k) for m in range(zs) for k in range(2)]
    count = len(steps)
    for step in range(count + 6):
        if step < count:
            line(*steps[step])
        if 0 <= step - 3 < count:
            cross(*steps[step - 3])
        if 0 <= step - 5 < count:
            corner(*steps[step - 5])
        if step == 6:
            for load in loads:
                load.wait()
        if 0 <= step - 6 < count and steps[step - 6][1]:
            multiply(steps[step - 6][0])
    for copy in started:
        copy.wait_send()


def encode(rows, w_proj, w_fc):
    tiles = lax.axis_size("tile")
    zs = tiles // CORES
    vmem = pl.BlockSpec(memory_space=pltpu.VMEM)
    hbm = pl.BlockSpec(memory_space=pltpu.HBM)
    dma = pltpu.SemaphoreType.DMA
    return pl.pallas_call(
        functools.partial(encode_kernel, tiles),
        out_shape=jax.ShapeDtypeStruct((rows.shape[0], w_fc.shape[1]), F32),
        in_specs=[hbm, vmem, hbm],
        out_specs=vmem,
        scratch_shapes=[
            pltpu.VMEM(rows.shape, BF),
            pltpu.VMEM(w_fc.shape, BF),
            pltpu.VMEM((rows.shape[1], w_proj.shape[1]), BF),
            pltpu.VMEM((rows.shape[0], w_proj.shape[1]), F32),
            dma((2,)),
            dma((zs, 2)),
            dma((zs, 2)),
            dma((2, zs, 2)),
            dma((2, zs, 2)),
            dma((zs, 2)),
            dma((zs, 2)),
            dma((4, zs, 2)),
            dma((4, zs, 2)),
        ],
        compiler_params=pltpu.CompilerParams(
            collective_id=0, has_side_effects=True, vmem_limit_bytes=61 << 20
        ),
        name="encode",
    )(rows, w_proj, w_fc)


def hops_kernel(tiles, cap, parts, list_ref, state_ref, adj_ref, self_ref, up_ref, down_ref, out_ref,
                state, terms, send0, own0, recv0, send1, recv1, send2, recv2, send3, recv3, agg,
                s0, r0, s1, r1, s2, r2, s3, r3):
    hops = up_ref.shape[0]
    zs = tiles // CORES
    far = zs // 2
    blocks, slots, tb, _ = adj_ref.shape
    width = state_ref.shape[1]
    sends = blocks * slots
    per = blocks // parts
    chunks = zs * parts
    sx = lax.axis_index("section")
    t = lax.axis_index("tile")
    z, c = t // CORES, t % CORES
    ox, oc = 1 - sx, 1 - c
    oz = z + 1 - 2 * (z % 2)
    partner = {"tile": z * CORES + oc}
    xn = {"section": ox}
    zn = {"tile": oz * CORES + c}

    def zdev(j):
        return {"tile": ((z + 2 * j) % zs) * CORES + c}

    order = []
    for j in range(1, far):
        order += [(oz + 2 * j) % zs, (z + 2 * j) % zs]
    order += [oz, z]

    wait = greet([partner, xn, zn] + [zdev(j) for j in range(1, far)])
    terms[sends] = jnp.zeros((tb, width), BF)
    state[...] = state_ref[...]

    def term(b, carry):
        nodes = state[pl.ds(pl.multiple_of(b * tb, tb), tb), :].astype(BF)
        whole = jnp.dot(adj_ref[b].reshape(slots * tb, tb), nodes, preferred_element_type=F32)
        terms[pl.ds(b * slots, slots)] = whole.astype(BF).reshape(slots, tb, width)
        agg[pl.ds(pl.multiple_of(b * tb, tb), tb), :] = jnp.dot(self_ref[b], nodes, preferred_element_type=F32)
        return carry

    lax.fori_loop(0, blocks, term, 0)
    wait()

    for hop in range(hops):
        pending = []

        def go(src, dst, ss, rs, device):
            copy = remote(src, dst, ss, rs, device)
            copy.start()
            pending.append(copy)

        def arrived(dst, ss, rs, device):
            remote(dst, dst, ss, rs, device).wait_recv()

        def sums(dst, x, q, core):
            i, h = divmod(q, parts)
            first = ((x * zs + order[i]) * CORES + core) * blocks + h * per

            def body(r, carry):
                base = (first + r) * cap
                total = terms[list_ref[base]].astype(F32)
                for j in range(1, cap):
                    total += terms[list_ref[base + j]].astype(F32)
                dst[r] = total.astype(BF)
                return carry

            lax.fori_loop(0, per, body, 0)

        def chip(k, q):
            x = (ox, sx)[k]
            sums(send0.at[k, q], x, q, oc)
            go(send0.at[k, q], recv0.at[hop, k, q], s0.at[hop, k, q], r0.at[hop, k, q], partner)
            sums(own0.at[k, q], x, q, c)

        def pair(q):
            arrived(recv0.at[hop, 0, q], s0.at[hop, 0, q], r0.at[hop, 0, q], partner)

            def body(r, carry):
                send1[q, r] = (own0[0, q, r].astype(F32) + recv0[hop, 0, q, r].astype(F32)).astype(BF)
                return carry

            lax.fori_loop(0, per, body, 0)
            go(send1.at[q], recv1.at[hop, q], s1.at[hop, q], r1.at[hop, q], xn)

        chip(0, 0)
        for q in range(1, chunks):
            chip(0, q)
            pair(q - 1)
        chip(1, 0)
        pair(chunks - 1)
        for q in range(1, chunks):
            chip(1, q)

        for q in range(chunks):
            i, h = divmod(q, parts)
            arrived(recv0.at[hop, 1, q], s0.at[hop, 1, q], r0.at[hop, 1, q], partner)
            arrived(recv1.at[hop, q], s1.at[hop, q], r1.at[hop, q], xn)
            slot = (i // 2) * parts + h
            onward = i % 2 == 0
            if not onward:
                arrived(recv2.at[hop, slot], s2.at[hop, slot], r2.at[hop, slot], zn)
            home = i == zs - 1

            def gathered(r):
                total = own0[1, q, r].astype(F32) + recv0[hop, 1, q, r].astype(F32)
                total += recv1[hop, q, r].astype(F32)
                return total if onward else total + recv2[hop, slot, r].astype(F32)

            if not home:
                out = send2 if onward else send3

                def body(r, carry):
                    out[slot, r] = gathered(r).astype(BF)
                    return carry

                lax.fori_loop(0, per, body, 0)
                if onward:
                    go(send2.at[slot], recv2.at[hop, slot], s2.at[hop, slot], r2.at[hop, slot], zn)
                else:
                    go(send3.at[slot], recv3.at[hop, slot], s3.at[hop, slot], r3.at[hop, slot], zdev(i // 2 + 1))
                continue
            for j in range(1, far):
                there = (j - 1) * parts + h
                arrived(recv3.at[hop, there], s3.at[hop, there], r3.at[hop, there], zdev(j))

            def finish(r, carry):
                rows = pl.ds(pl.multiple_of((h * per + r) * tb, tb), tb)
                total = agg[rows, :] + gathered(r)
                for j in range(1, far):
                    total += recv3[hop, (j - 1) * parts + h, r].astype(F32)
                inner = jnp.dot(total.astype(BF), up_ref[hop], preferred_element_type=F32)
                inner = jnp.maximum(inner, 0.0).astype(BF)
                after = state[rows, :] + jnp.dot(inner, down_ref[hop], preferred_element_type=F32)
                if hop == hops - 1:
                    out_ref[rows, :] = after.astype(BF)
                else:
                    state[rows, :] = after
                return carry

            lax.fori_loop(0, per, finish, 0, unroll=True)
            if hop < hops - 1:
                lax.fori_loop(h * per, h * per + per, term, 0)
        for copy in pending:
            copy.wait_send()


def graph(state, adjacency, self_adj, w_up, w_down, lists, cap):
    tiles = lax.axis_size("tile")
    zs = tiles // CORES
    far = zs // 2
    blocks, slots, tb, _ = adjacency.shape
    width = state.shape[1]
    hops = w_up.shape[0]
    parts = PARTS if blocks % PARTS == 0 else 1
    piece = (blocks // parts, tb, width)
    chunks = zs * parts
    onward = far * parts
    distant = max(1, (far - 1) * parts)
    vmem = pl.BlockSpec(memory_space=pltpu.VMEM)
    dma = pltpu.SemaphoreType.DMA
    return pl.pallas_call(
        functools.partial(hops_kernel, tiles, cap, parts),
        out_shape=jax.ShapeDtypeStruct(state.shape, BF),
        in_specs=[pl.BlockSpec(memory_space=pltpu.SMEM)] + [vmem] * 5,
        out_specs=vmem,
        scratch_shapes=[
            pltpu.VMEM(state.shape, F32),
            pltpu.VMEM((blocks * slots + 1, tb, width), BF),
            pltpu.VMEM((2, chunks) + piece, BF),
            pltpu.VMEM((2, chunks) + piece, BF),
            pltpu.VMEM((hops, 2, chunks) + piece, BF),
            pltpu.VMEM((chunks,) + piece, BF),
            pltpu.VMEM((hops, chunks) + piece, BF),
            pltpu.VMEM((onward,) + piece, BF),
            pltpu.VMEM((hops, onward) + piece, BF),
            pltpu.VMEM((distant,) + piece, BF),
            pltpu.VMEM((hops, distant) + piece, BF),
            pltpu.VMEM(state.shape, F32),
        ]
        + [dma((hops, 2, chunks))] * 2
        + [dma((hops, chunks))] * 2
        + [dma((hops, onward))] * 2
        + [dma((hops, distant))] * 2,
        compiler_params=pltpu.CompilerParams(
            collective_id=1, has_side_effects=True, vmem_limit_bytes=50 << 20
        ),
        name="hops",
    )(lists, state, adjacency, self_adj, w_up, w_down)


def entry_lists(targets, live, total_blocks, cap):
    sends = targets.shape[0]
    positions = jnp.arange(sends, dtype=jnp.int32)
    same = (targets[:, None] == targets[None, :]) & live[None, :] & (positions[None, :] < positions[:, None])
    rank = jnp.sum(same.astype(jnp.int32), axis=1)
    hit = (jnp.arange(total_blocks, dtype=jnp.int32)[:, None, None] == targets[None, None, :]) & live[None, None, :]
    hit = hit & (jnp.arange(cap, dtype=jnp.int32)[None, :, None] == rank[None, None, :])
    found = jnp.sum(jnp.where(hit, positions[None, None, :] - sends, 0), axis=2) + sends
    return found.reshape(total_blocks * cap)


def local(features, w_proj, w_fc, w_up, w_down, self_adj, adjacency, nbr_block, counts):
    rows = features[0]
    blocks = self_adj.shape[1]
    tb = self_adj.shape[2]
    width = w_fc.shape[1]
    slots = adjacency.shape[2]
    hops = w_up.shape[0]
    pairs = lax.axis_size("section") == 2 and lax.axis_size("tile") % (2 * CORES) == 0
    peers = lax.axis_size("section") * lax.axis_size("tile")
    me_index = lax.axis_index("section") * lax.axis_size("tile") + lax.axis_index("tile")
    sends = blocks * slots
    cap = (sends + peers - 1) // peers
    if pairs and lax.axis_size("slide") == 2 and w_proj.shape[0] % 32 == 0:
        state = encode(rows, w_proj, w_fc)
    else:
        pre = jnp.dot(
            rows,
            lax.all_gather(w_proj, ("section", "tile", "slide"), axis=0, tiled=True),
            preferred_element_type=F32,
        )
        encoded = jax.nn.relu(pre).astype(BF)
        state = jnp.dot(encoded, w_fc, preferred_element_type=F32)
    live = jnp.arange(slots, dtype=jnp.int32)[None, :] < counts[0][:, None]
    if pairs and blocks <= CORES * cap:
        targets = lax.dynamic_slice_in_dim(nbr_block[0], me_index * blocks, blocks, 0).reshape(sends)
        lists = entry_lists(targets, live.reshape(sends), peers * blocks, cap)
        return graph(state, adjacency[0], self_adj[0], w_up, w_down, lists, cap)[None]
    table = nbr_block[0].reshape(peers, sends)
    target_dev = table // blocks
    target_local = table % blocks
    positions = jnp.arange(sends, dtype=jnp.int32)
    before = positions[None, :] < positions[:, None]
    same = target_dev[:, :, None] == target_dev[:, None, :]
    ranking = jnp.sum(jnp.logical_and(same, before[None]).astype(jnp.int32), axis=2)
    mine_dev = lax.dynamic_index_in_dim(target_dev, me_index, 0, keepdims=False)
    mine_rank = lax.dynamic_index_in_dim(ranking, me_index, 0, keepdims=False)
    slot_of = mine_dev * cap + mine_rank
    send_map = (jnp.arange(peers * cap, dtype=jnp.int32)[:, None] == slot_of[None, :]).astype(BF)
    arrive_hit = target_dev == me_index
    slot_flags = jnp.logical_and(
        arrive_hit[:, :, None],
        ranking[:, :, None] == jnp.arange(cap, dtype=jnp.int32)[None, None, :],
    ).astype(F32)
    local_flags = (
        target_local[:, :, None] == jnp.arange(blocks, dtype=jnp.int32)[None, None, :]
    ).astype(F32)
    recv_map = (
        jnp.einsum("pjc,pjr->rpc", slot_flags, local_flags).reshape(blocks, peers * cap).astype(BF)
    )
    for hop in range(hops):
        nodes = state.astype(BF).reshape(blocks, tb, width)
        own = jnp.einsum("bij,bjh->bih", self_adj[0], nodes, preferred_element_type=F32)
        terms = jnp.einsum("bkij,bjh->bkih", adjacency[0], nodes, preferred_element_type=F32)
        terms = (
            jnp.where(live[:, :, None, None], terms, 0.0).astype(BF).reshape(sends, tb * width)
        )
        outgoing = jnp.dot(send_map, terms, preferred_element_type=F32).astype(BF)
        outgoing = outgoing.reshape(peers, cap, tb, width)
        arrived = lax.all_to_all(
            outgoing, ("section", "tile"), split_axis=0, concat_axis=0, tiled=True
        )
        arrived = arrived.reshape(peers * cap, tb * width)
        incoming = jnp.dot(recv_map, arrived, preferred_element_type=F32).reshape(
            blocks, tb, width
        )
        gathered = (own + incoming).astype(BF).reshape(blocks * tb, width)
        inner = jax.nn.relu(jnp.dot(gathered, w_up[hop], preferred_element_type=F32)).astype(BF)
        state = state + jnp.dot(inner, w_down[hop], preferred_element_type=F32)
    return state.astype(BF)[None]


def solution(mesh):
    return jax.shard_map(
        local,
        mesh=mesh,
        in_specs=(
            P("slide", ("section", "tile"), None),
            P(("section", "tile", "slide"), None),
            P(),
            P(),
            P(),
            P("slide", ("section", "tile"), None, None),
            P("slide", ("section", "tile"), None, None, None),
            P("slide", None, None),
            P("slide", ("section", "tile")),
        ),
        out_specs=P("slide", ("section", "tile"), None),
        check_vma=False,
    )
```
